32 devices in a mesh: fsdp: 8 (over z, y), tp: 4 (over x, core).
Axes of the slice: x: 2, y: 2, z: 4, core: 2. Of those that a mesh axis runs over, the one named last changes fastest.
Arguments:
- tokens: bfloat16 [8192, 1536], P(('fsdp', 'tp')), may hold values from -6 to 6
- seq_starts: int32 [8192], P('fsdp'), may hold values from 0 to 1023, as said below
- attn_gain: float32 [1536], replicated, may hold values from 0.5 to 1.5
- query_weight: bfloat16 [1536, 1536], P('fsdp', 'tp'), may hold values from -0.15625 to 0.15625
- query_bias: float32 [1536], P('tp'), may hold values from -8 to 8
- keyval_weight: bfloat16 [1536, 512], P(('fsdp', 'tp')), may hold values from -0.15625 to 0.15625
- keyval_bias: float32 [512], replicated, may hold values from -8 to 8
- out_weight: bfloat16 [1536, 1536], P('tp', 'fsdp'), may hold values from -0.5 to 0.5
- mlp_gain: float32 [1536], replicated, may hold values from 0.5 to 1.5
- gate_weight: bfloat16 [1536, 8960], P('fsdp', 'tp'), may hold values from -0.15625 to 0.15625
- up_weight: bfloat16 [1536, 8960], P('fsdp', 'tp'), may hold values from -0.15625 to 0.15625
- down_weight: bfloat16 [8960, 1536], P('tp', 'fsdp'), may hold values from -0.125 to 0.125
- cotangent: bfloat16 [8192, 1536], P(('fsdp', 'tp')), may hold values from -6 to 6
Outputs:
- output: bfloat16 [8192, 1536], P(('fsdp', 'tp'))
- input_grad: float32 [8192, 1536], P(('fsdp', 'tp'))
- attn_gain_grad: float32 [1536], replicated
- query_weight_grad: float32 [1536, 1536], P('fsdp', 'tp')
- query_bias_grad: float32 [1536], P('tp')
- keyval_weight_grad: float32 [1536, 512], P(('fsdp', 'tp'))
- keyval_bias_grad: float32 [512], replicated
- out_weight_grad: float32 [1536, 1536], P('tp', 'fsdp')
- mlp_gain_grad: float32 [1536], replicated
- gate_weight_grad: float32 [1536, 8960], P('fsdp', 'tp')
- up_weight_grad: float32 [1536, 8960], P('fsdp', 'tp')
- down_weight_grad: float32 [8960, 1536], P('tp', 'fsdp')
The draws below stay inside these ranges and needn't reach their ends.
Inputs may be any that keep to these rules, and one draw needn't show every extreme that they name: `seq_starts`: sequences are runs of consecutive tokens inside a block of 1024 tokens, each of at most 512 tokens; every block begins with one of exactly 512 tokens.
All inputs are finite; a program needn't handle non-finite values.
Results may differ from the reference program's by a relative error of at most 0.035.
The reference program's roundings to bfloat16 on the way (of `normed_first`, `probs`, `attn_out`, `normed_second`, `hidden` and `grad_scores`) count: a program that leaves them out, or rounds other values in their place, can miss the bound.
Values may be sent and summed in bfloat16 or wider, within the bound.
No kernel may reach another device: no remote copies, remote signals or barrier semaphores. Data moves between devices by JAX's collectives and lax.ppermute only.
A program may use at most 256 MiB of HBM per device.

```python
import jax
import jax.numpy as jnp
from jax import lax

D = 1536
H = 12
KV = 2
HD = 128
FF = 8960
SEG_MAX = 512
TOK_GRP = 1024
TOKENS = 8192
N_FSDP = 8
N_TP = 4


def draw_seq_starts(key, part):
    lowest = max(1, SEG_MAX // 8)
    pieces = TOK_GRP // lowest + 1
    group_count = TOKENS // TOK_GRP
    lengths = jax.random.randint(key, (group_count, pieces), lowest, SEG_MAX + 1)
    lengths = jnp.where(jnp.arange(pieces)[None, :] == 0, SEG_MAX, lengths)
    bounds = jnp.cumsum(lengths, axis=1)
    places = jnp.arange(TOK_GRP)
    below = bounds[:, None, :] <= places[None, :, None]
    starts = jnp.max(jnp.where(below, bounds[:, None, :], 0), axis=2)
    starts = starts.at[0, TOK_GRP - 1].set(TOK_GRP - 1)
    return starts.reshape(-1).astype(jnp.int32)


def draw_query_bias(key, part):
    values = jnp.clip(0.5 * jax.random.normal(key, (H * HD,), jnp.float32), -2.0, 2.0)
    return values


def draw_keyval_bias(key, part):
    values = jnp.clip(0.5 * jax.random.normal(key, (2 * KV * HD,), jnp.float32), -2.0, 2.0)
    return values


def shard_levels(rng, shape, cuts, low, top_value):
    loudness, own = 1.0, jax.random.fold_in(rng, 6)
    for position, blocks in cuts:
        steps = jnp.exp(jax.random.uniform(jax.random.fold_in(own, position), (blocks,), jnp.float32, low / len(cuts), top_value / len(cuts)))
        loudness = loudness * jnp.repeat(steps, shape[position] // blocks).reshape([-1 if axis == position else 1 for axis in range(len(shape))])
    return loudness


def centred(rng, dims, width, bound, cuts=(), kind=jnp.bfloat16):
    values = jax.random.normal(rng, dims, jnp.float32) * width
    if len(cuts) > 0:
        values = shard_levels(rng, dims, cuts, -0.22, 0.18) * values
    return jnp.clip(values, min=-bound, max=bound).astype(kind)


def setup_inputs(seed: int = 0) -> dict:
    arg_keys = jax.random.split(jax.random.key(seed), 14)
    tokens = centred(arg_keys[0], (TOKENS, D), 1.0, 6.0, ((0, 32),))
    seq_starts = draw_seq_starts(jax.random.fold_in(arg_keys[13], 71), 0)
    attn_gain = jnp.clip(1.0 + 0.1 * jax.random.normal(arg_keys[2], (D,), jnp.float32), 0.5, 1.5)
    query_weight = centred(arg_keys[3], (D, H * HD), D ** -0.5, 0.15625, ((0, 8), (1, 4)))
    query_bias = draw_query_bias(jax.random.fold_in(arg_keys[13], 71), 0)
    keyval_weight = centred(arg_keys[5], (D, 2 * KV * HD), D ** -0.5, 0.15625, ((0, 32),))
    keyval_bias = draw_keyval_bias(jax.random.fold_in(arg_keys[13], 71), 0)
    out_weight = centred(arg_keys[7], (H * HD, D), HD ** -0.5, 0.5, ((0, 4), (1, 8)))
    mlp_gain = jnp.clip(1.0 + 0.1 * jax.random.normal(arg_keys[8], (D,), jnp.float32), 0.5, 1.5)
    gate_weight = centred(arg_keys[9], (D, FF), D ** -0.5, 0.15625, ((0, 8), (1, 4)))
    up_weight = centred(arg_keys[10], (D, FF), D ** -0.5, 0.15625, ((0, 8), (1, 4)))
    down_weight = centred(arg_keys[11], (FF, D), (FF // 4) ** -0.5, 0.125, ((0, 4), (1, 8)))
    cotangent = centred(arg_keys[12], (TOKENS, D), 1.0, 6.0, ((0, 32),))
    return {"tokens": tokens, "seq_starts": seq_starts, "attn_gain": attn_gain, "query_weight": query_weight, "query_bias": query_bias, "keyval_weight": keyval_weight, "keyval_bias": keyval_bias, "out_weight": out_weight, "mlp_gain": mlp_gain, "gate_weight": gate_weight, "up_weight": up_weight, "down_weight": down_weight, "cotangent": cotangent}


NORM_EPSILON = 1e-06
ROPE_THETA = 1000000.0
MASKED_SCORE = -1e+30

def product(form, left, right):
    return jnp.einsum(form, left.astype(jnp.float32), right.astype(jnp.float32))

def matmul(left, right):
    return jnp.dot(left, right, preferred_element_type=jnp.float32)

def rotary_tables(positions):
    exponent = jnp.arange(HD // 2, dtype=jnp.float32) * 2.0 / HD
    frequency = ROPE_THETA ** (-exponent)
    angles = positions.astype(jnp.float32)[:, None] * frequency[None, :]
    angles = jnp.concatenate([angles, angles], axis=1)
    return (jnp.cos(angles), jnp.sin(angles))

def rotate(values, cosine, sine):
    half_dim = HD // 2
    turned = jnp.concatenate([-values[..., half_dim:], values[..., :half_dim]], axis=-1)
    return values * cosine[:, None, :] + turned * sine[:, None, :]

def rotate_back(grads, cosine, sine):
    half_dim = HD // 2
    scaled = grads * sine[:, None, :]
    turned = jnp.concatenate([scaled[..., half_dim:], -scaled[..., :half_dim]], axis=-1)
    return grads * cosine[:, None, :] + turned

def padded(key_rows, value_rows, starts):
    pad_keys = jnp.concatenate([jnp.zeros((SEG_MAX, HD), key_rows.dtype), key_rows], axis=0)
    pad_values = jnp.concatenate([jnp.zeros((SEG_MAX, HD), value_rows.dtype), value_rows], axis=0)
    pad_starts = jnp.concatenate([jnp.full((SEG_MAX,), -1, jnp.int32), starts.astype(jnp.int32)], axis=0)
    return (pad_keys, pad_values, pad_starts)

def block_scores(query, pad_keys, pad_values, starts, pad_starts, block_index):
    block_start = block_index * SEG_MAX
    query_block = lax.dynamic_slice_in_dim(query, block_start, SEG_MAX, 0)
    key_block = lax.dynamic_slice_in_dim(pad_keys, block_start, 2 * SEG_MAX, 0)
    value_block = lax.dynamic_slice_in_dim(pad_values, block_start, 2 * SEG_MAX, 0)
    query_starts = lax.dynamic_slice_in_dim(starts.astype(jnp.int32), block_start, SEG_MAX, 0)
    key_starts = lax.dynamic_slice_in_dim(pad_starts, block_start, 2 * SEG_MAX, 0)
    row_ids = block_start + jnp.arange(SEG_MAX, dtype=jnp.int32)
    col_ids = block_start - SEG_MAX + jnp.arange(2 * SEG_MAX, dtype=jnp.int32)
    allowed = (query_starts[:, None] == key_starts[None, :]) & (col_ids[None, :] <= row_ids[:, None])
    scores = product('qrd,kd->rqk', query_block, key_block) * HD ** (-0.5)
    scores = jnp.where(allowed[None, :, :], scores, MASKED_SCORE)
    return (query_block, key_block, value_block, scores)

def attend(query, key_rows, value_rows, starts):
    row_count = query.shape[0]
    pad_keys, pad_values, pad_starts = padded(key_rows, value_rows, starts)

    def forward_block(block_index):
        query_block, key_block, value_block, scores = block_scores(query, pad_keys, pad_values, starts, pad_starts, block_index)
        row_max = lax.optimization_barrier(jnp.max(scores, axis=-1, keepdims=True))
        weights = jnp.exp(scores - row_max)
        totals = lax.optimization_barrier(jnp.sum(weights, axis=-1, keepdims=True))
        probs = (weights / totals).astype(jnp.bfloat16)
        result = product('rqk,kd->qrd', probs, value_block).astype(jnp.bfloat16)
        return (result, (row_max + jnp.log(totals))[..., 0])
    results, log_totals = lax.map(forward_block, jnp.arange(row_count // SEG_MAX, dtype=jnp.int32))
    return (results.reshape(row_count, query.shape[1], HD), log_totals)

def attend_back(query, key_rows, value_rows, starts, results, log_totals, grad_out):
    row_count = query.shape[0]
    pad_keys, pad_values, pad_starts = padded(key_rows, value_rows, starts)
    row_delta = lax.optimization_barrier(jnp.sum(results.astype(jnp.float32) * grad_out.astype(jnp.float32), axis=-1))

    def back_block(running, block_index):
        key_accum, value_accum = running
        query_block, key_block, value_block, scores = block_scores(query, pad_keys, pad_values, starts, pad_starts, block_index)
        block_start = block_index * SEG_MAX
        probs = jnp.exp(scores - log_totals[block_index][:, :, None])
        grad_block = lax.dynamic_slice_in_dim(grad_out, block_start, SEG_MAX, 0)
        delta_block = lax.dynamic_slice_in_dim(row_delta, block_start, SEG_MAX, 0)
        value_part = product('rqk,qrd->kd', probs.astype(jnp.bfloat16), grad_block)
        grad_probs = product('qrd,kd->rqk', grad_block, value_block)
        grad_scores = (probs * (grad_probs - jnp.transpose(delta_block)[:, :, None]) * HD ** (-0.5)).astype(jnp.bfloat16)
        query_part = product('rqk,kd->qrd', grad_scores, key_block)
        key_part = product('rqk,qrd->kd', grad_scores, query_block)
        key_accum = lax.dynamic_update_slice_in_dim(key_accum, lax.dynamic_slice_in_dim(key_accum, block_start, 2 * SEG_MAX, 0) + key_part, block_start, 0)
        value_accum = lax.dynamic_update_slice_in_dim(value_accum, lax.dynamic_slice_in_dim(value_accum, block_start, 2 * SEG_MAX, 0) + value_part, block_start, 0)
        return ((key_accum, value_accum), query_part)
    empty = jnp.zeros((row_count + SEG_MAX, HD), jnp.float32)
    (key_accum, value_accum), query_parts = lax.scan(back_block, (empty, empty), jnp.arange(row_count // SEG_MAX, dtype=jnp.int32))
    return (query_parts.reshape(row_count, query.shape[1], HD), key_accum[SEG_MAX:], value_accum[SEG_MAX:])

def group_pass(params, tokens, seq_starts, cotangent):
    attn_gain, query_weight, query_bias, keyval_weight, keyval_bias, out_weight, mlp_gain, gate_weight, up_weight, down_weight = params
    row_count = tokens.shape[0]
    heads_dev = H // N_TP
    group_size = H // KV
    positions = jnp.arange(row_count, dtype=jnp.int32) - seq_starts.astype(jnp.int32)
    cosine, sine = rotary_tables(positions)
    stream_in = tokens.astype(jnp.float32)
    scale_first = lax.rsqrt(lax.optimization_barrier(jnp.mean(stream_in * stream_in, axis=-1, keepdims=True)) + NORM_EPSILON)
    unit_first = stream_in * scale_first
    normed_first = (unit_first * attn_gain).astype(jnp.bfloat16)
    query_lin = matmul(normed_first, query_weight) + query_bias
    keyval_lin = matmul(normed_first, keyval_weight) + keyval_bias
    query = rotate(query_lin.reshape(row_count, H, HD), cosine, sine).astype(jnp.bfloat16)
    key_rows = rotate(keyval_lin[:, :KV * HD].reshape(row_count, KV, HD), cosine, sine).astype(jnp.bfloat16)
    value_rows = keyval_lin[:, KV * HD:].reshape(row_count, KV, HD).astype(jnp.bfloat16)
    results = []
    totals_list = []
    for share_index in range(N_TP):
        kv_head = share_index * heads_dev // group_size
        share_out, share_totals = attend(query[:, share_index * heads_dev:(share_index + 1) * heads_dev], key_rows[:, kv_head], value_rows[:, kv_head], seq_starts)
        results.append(share_out)
        totals_list.append(share_totals)
    attn_out = jnp.concatenate(results, axis=1).reshape(row_count, H * HD)
    middle = stream_in + matmul(attn_out, out_weight)
    scale_second = lax.rsqrt(lax.optimization_barrier(jnp.mean(middle * middle, axis=-1, keepdims=True)) + NORM_EPSILON)
    unit_second = middle * scale_second
    normed_second = (unit_second * mlp_gain).astype(jnp.bfloat16)
    gate_lin = matmul(normed_second, gate_weight)
    up_lin = matmul(normed_second, up_weight)
    sigmoid_gate = jax.nn.sigmoid(gate_lin)
    silu_gate = gate_lin * sigmoid_gate
    hidden = (silu_gate * up_lin).astype(jnp.bfloat16)
    output = (middle + matmul(hidden, down_weight)).astype(jnp.bfloat16)
    grad_hidden = matmul(cotangent, down_weight.T)
    down_weight_grad = matmul(hidden.T, cotangent)
    grad_gate = (grad_hidden * up_lin * sigmoid_gate * (1.0 + gate_lin * (1.0 - sigmoid_gate))).astype(jnp.bfloat16)
    grad_up = (grad_hidden * silu_gate).astype(jnp.bfloat16)
    grad_second = matmul(grad_gate, gate_weight.T) + matmul(grad_up, up_weight.T)
    gate_weight_grad = matmul(normed_second.T, grad_gate)
    up_weight_grad = matmul(normed_second.T, grad_up)
    mlp_gain_grad = lax.optimization_barrier(jnp.sum(grad_second * unit_second, axis=0))
    weighted_second = mlp_gain * grad_second
    grad_middle = cotangent.astype(jnp.float32) + scale_second * (weighted_second - unit_second * lax.optimization_barrier(jnp.mean(weighted_second * unit_second, axis=-1, keepdims=True)))
    grad_mid_low = grad_middle.astype(jnp.bfloat16)
    grad_attn = matmul(grad_mid_low, out_weight.T).astype(jnp.bfloat16).reshape(row_count, H, HD)
    out_weight_grad = matmul(attn_out.T, grad_mid_low)
    grad_first = jnp.zeros((row_count, D), jnp.float32)
    keyval_weight_grad = jnp.zeros((D, 2 * KV * HD), jnp.float32)
    keyval_bias_grad = jnp.zeros((2 * KV * HD,), jnp.float32)
    query_grads = []
    for share_index in range(N_TP):
        kv_head = share_index * heads_dev // group_size
        head_span = slice(share_index * heads_dev, (share_index + 1) * heads_dev)
        share_query, share_key, share_value = attend_back(query[:, head_span], key_rows[:, kv_head], value_rows[:, kv_head], seq_starts, results[share_index], totals_list[share_index], grad_attn[:, head_span])
        query_grads.append(rotate_back(share_query, cosine, sine))
        key_pre = rotate_back(share_key[:, None, :], cosine, sine)[:, 0]
        share_keyval = jnp.concatenate([key_pre, share_value], axis=1)
        share_low = share_keyval.astype(jnp.bfloat16)
        key_cols = slice(kv_head * HD, (kv_head + 1) * HD)
        value_cols = slice(KV * HD + kv_head * HD, KV * HD + (kv_head + 1) * HD)
        head_weight = jnp.concatenate([keyval_weight[:, key_cols], keyval_weight[:, value_cols]], axis=1)
        grad_first = grad_first + matmul(share_low, head_weight.T)
        head_grad = matmul(normed_first.T, share_low)
        keyval_weight_grad = keyval_weight_grad.at[:, key_cols].add(head_grad[:, :HD]).at[:, value_cols].add(head_grad[:, HD:])
        head_bias = lax.optimization_barrier(jnp.sum(share_keyval, axis=0))
        keyval_bias_grad = keyval_bias_grad.at[key_cols].add(head_bias[:HD]).at[value_cols].add(head_bias[HD:])
    query_pre = jnp.concatenate(query_grads, axis=1).reshape(row_count, H * HD)
    query_low = query_pre.astype(jnp.bfloat16)
    grad_first = grad_first + matmul(query_low, query_weight.T)
    query_weight_grad = matmul(normed_first.T, query_low)
    query_bias_grad = lax.optimization_barrier(jnp.sum(query_pre, axis=0))
    attn_gain_grad = lax.optimization_barrier(jnp.sum(grad_first * unit_first, axis=0))
    weighted_first = attn_gain * grad_first
    input_grad = grad_middle + scale_first * (weighted_first - unit_first * lax.optimization_barrier(jnp.mean(weighted_first * unit_first, axis=-1, keepdims=True)))
    grads = (attn_gain_grad, query_weight_grad, query_bias_grad, keyval_weight_grad, keyval_bias_grad, out_weight_grad, mlp_gain_grad, gate_weight_grad, up_weight_grad, down_weight_grad)
    return (output, input_grad, grads)

def add_pair(first_grad, second_grad):
    return first_grad + second_grad

def reference(tokens, seq_starts, attn_gain, query_weight, query_bias, keyval_weight, keyval_bias, out_weight, mlp_gain, gate_weight, up_weight, down_weight, cotangent):
    params = (attn_gain, query_weight, query_bias, keyval_weight, keyval_bias, out_weight, mlp_gain, gate_weight, up_weight, down_weight)

    def group_step(running, inputs):
        group_tokens, group_starts, group_cot = inputs
        output, input_grad, grads = group_pass(params, group_tokens, group_starts, group_cot)
        return (jax.tree.map(add_pair, running, grads), (output, input_grad))
    zeros = tuple((jnp.zeros(param_item.shape, jnp.float32) for param_item in params))
    inputs = (tokens.reshape(N_FSDP, TOK_GRP, D), seq_starts.reshape(N_FSDP, TOK_GRP), cotangent.reshape(N_FSDP, TOK_GRP, D))
    grads, (outputs, input_grads) = lax.scan(group_step, zeros, inputs)
    return (outputs.reshape(TOKENS, D), input_grads.reshape(TOKENS, D), grads[0], grads[1], grads[2], grads[3], grads[4], grads[5], grads[6], grads[7], grads[8], grads[9])
```

```python
import jax
import jax.numpy as jnp
from jax import lax
from jax.sharding import PartitionSpec as P

H = 12
KV = 2
HD = 128
SEG_MAX = 512

NORM_EPSILON = 1e-06
ROPE_THETA = 1000000.0
MASKED_SCORE = -1e30


def product(form, left, right):
    return jnp.einsum(form, left, right, preferred_element_type=jnp.float32)


def matmul(left, right):
    return jnp.dot(left, right, preferred_element_type=jnp.float32)


def rotary_tables(positions):
    exponent = jnp.arange(HD // 2, dtype=jnp.float32) * 2.0 / HD
    frequency = ROPE_THETA ** (-exponent)
    angles = positions.astype(jnp.float32)[:, None] * frequency[None, :]
    angles = jnp.concatenate([angles, angles], axis=1)
    return (jnp.cos(angles), jnp.sin(angles))


def rotate(values, cosine, sine):
    half_dim = HD // 2
    turned = jnp.concatenate([-values[..., half_dim:], values[..., :half_dim]], axis=-1)
    return values * cosine[:, None, :] + turned * sine[:, None, :]


def rotate_back(grads, cosine, sine):
    half_dim = HD // 2
    scaled = grads * sine[:, None, :]
    turned = jnp.concatenate([scaled[..., half_dim:], -scaled[..., :half_dim]], axis=-1)
    return grads * cosine[:, None, :] + turned


def scores_of(query, key_rows, allowed):
    scores = product("bqrd,bkd->brqk", query, key_rows) * HD ** (-0.5)
    return jnp.where(allowed[:, None], scores, MASKED_SCORE)


def attend(query, key_rows, value_rows, allowed):
    scores = scores_of(query, key_rows, allowed)
    row_max = jnp.max(scores, axis=-1, keepdims=True)
    weights = jnp.exp(scores - row_max)
    totals = jnp.sum(weights, axis=-1, keepdims=True)
    probs = (weights / totals).astype(jnp.bfloat16)
    result = product("brqk,bkd->bqrd", probs, value_rows).astype(jnp.bfloat16)
    return result, row_max + jnp.log(totals)


def attend_back(query, key_rows, value_rows, allowed, results, log_totals, grad_out):
    row_delta = jnp.sum(results.astype(jnp.float32) * grad_out.astype(jnp.float32), axis=-1)
    scores = scores_of(query, key_rows, allowed)
    probs = jnp.exp(scores - log_totals)
    value_grad = product("brqk,bqrd->bkd", probs.astype(jnp.bfloat16), grad_out)
    grad_probs = product("bqrd,bkd->brqk", grad_out, value_rows)
    grad_scores = (
        probs * (grad_probs - jnp.transpose(row_delta, (0, 2, 1))[..., None]) * HD ** (-0.5)
    ).astype(jnp.bfloat16)
    query_grad = product("brqk,bkd->bqrd", grad_scores, key_rows)
    key_grad = product("brqk,bqrd->bkd", grad_scores, query)
    return query_grad, key_grad, value_grad


def make_local(n_fsdp, n_tp):
    pairs = n_fsdp // 2
    other = [(i, i ^ 1) for i in range(n_fsdp)]

    def pull(k):
        return [
            (2 * ((z + k) % pairs) + y, 2 * z + y) for z in range(pairs) for y in range(2)
        ]

    def push(k):
        return [
            (2 * z + y, 2 * ((z + k) % pairs) + y) for z in range(pairs) for y in range(2)
        ]

    core_swap = [(i, i ^ 1) for i in range(n_tp)]
    chip_swap = [(i, i ^ 2) for i in range(n_tp)]

    def send(value, axis, perm):
        return lax.ppermute(value, axis, perm)

    def gather_weights(shard):
        same = [shard] + [send(shard, "fsdp", pull(k)) for k in range(1, pairs)]
        across = [send(piece, "fsdp", other) for piece in same]
        return jnp.concatenate(same + across, axis=0)

    def scatter_grads(rows_t, cols, rows):
        def part(index):
            return matmul(rows_t[index * rows : (index + 1) * rows], cols)

        order = list(range(1, pairs)) + [0]
        arrived = {
            k: send(part(pairs + k).astype(jnp.bfloat16), "fsdp", other) for k in order
        }
        moved = [
            send(
                (part(k) + arrived[k].astype(jnp.float32)).astype(jnp.bfloat16), "fsdp", push(k)
            )
            for k in order[:-1]
        ]
        total = part(0) + arrived[0].astype(jnp.float32)
        for piece in moved:
            total = total + piece.astype(jnp.float32)
        return total

    def spread(rows):
        near = send(rows, "tp", core_swap)
        far = send(rows, "tp", chip_swap)
        return jnp.concatenate([rows, near, far, send(far, "tp", core_swap)], axis=0)

    def collect(partial_sum):
        size = partial_sum.shape[0] // n_tp
        own, near, far, across = (partial_sum[i * size : (i + 1) * size] for i in range(n_tp))
        far = far + send(across, "tp", core_swap)
        moved = send(far.astype(jnp.bfloat16), "tp", chip_swap)
        return own + send(near, "tp", core_swap) + moved.astype(jnp.float32)

    def local(
        tokens,
        seq_starts,
        attn_gain,
        query_weight,
        query_bias,
        keyval_weight,
        keyval_bias,
        out_weight,
        mlp_gain,
        gate_weight,
        up_weight,
        down_weight,
        cotangent,
    ):
        width = tokens.shape[1]
        rows = width // n_fsdp
        heads_dev = query_weight.shape[1] // HD
        row_count = seq_starts.shape[0]
        own_rows = row_count // n_tp
        tp_index = lax.axis_index("tp")
        fsdp_index = lax.axis_index("fsdp")
        pair, side = fsdp_index // 2, fsdp_index % 2
        chip = tp_index // 2
        blocks = [
            2 * ((pair + k) % pairs) + (side if o == 0 else 1 - side)
            for o in range(2)
            for k in range(pairs)
        ]

        def to_local(x):
            return jnp.concatenate(
                [lax.dynamic_slice_in_dim(x, b * rows, rows, x.ndim - 1) for b in blocks], axis=-1
            )

        def from_local(x):
            out = jnp.zeros_like(x)
            for i, b in enumerate(blocks):
                out = lax.dynamic_update_slice_in_dim(
                    out, x[..., i * rows : (i + 1) * rows], b * rows, x.ndim - 1
                )
            return out

        def head_columns(x, head):
            return jnp.concatenate(
                [
                    lax.dynamic_slice_in_dim(x, head * HD, HD, x.ndim - 1),
                    lax.dynamic_slice_in_dim(x, (KV + head) * HD, HD, x.ndim - 1),
                ],
                axis=-1,
            )

        kv_head = tp_index * heads_dev // (H // KV)
        kv_near = send(keyval_weight, "tp", core_swap)
        kv_far = send(keyval_weight, "tp", chip_swap)
        kv_across = send(kv_far, "tp", core_swap)
        kv_stack = jnp.stack([keyval_weight, kv_near, kv_far, kv_across])
        kv_rows = jnp.concatenate(
            [
                lax.dynamic_index_in_dim(kv_stack, tp_index ^ i, 0, keepdims=False)
                for i in range(n_tp)
            ],
            axis=0,
        )
        head_bias = head_columns(keyval_bias, kv_head)
        q_width = query_weight.shape[1]
        first_shard = jnp.concatenate(
            [query_weight, head_columns(kv_rows, kv_head), out_weight.T], axis=1
        )
        first_full = gather_weights(first_shard)
        query_full = first_full[:, :q_width]
        head_full = first_full[:, q_width : q_width + 2 * HD]
        out_full_t = first_full[:, q_width + 2 * HD :]
        gate_full = gather_weights(gate_weight)
        up_full = gather_weights(up_weight)
        down_full_t = gather_weights(down_weight.T)

        order = [tp_index ^ i for i in range(n_tp)]
        starts = jnp.concatenate(
            [lax.dynamic_slice_in_dim(seq_starts, o * own_rows, own_rows, 0) for o in order]
        )
        places = jnp.concatenate(
            [o * own_rows + jnp.arange(own_rows, dtype=jnp.int32) for o in order]
        )
        cosine, sine = rotary_tables(places - starts)
        half = row_count // SEG_MAX
        starts_2, places_2 = starts.reshape(half, SEG_MAX), places.reshape(half, SEG_MAX)
        allowed = (starts_2[:, :, None] == starts_2[:, None, :]) & (
            places_2[:, None, :] <= places_2[:, :, None]
        )

        stream_in = to_local(tokens).astype(jnp.float32)
        cot = to_local(cotangent)
        attn_gain_l, mlp_gain_l = to_local(attn_gain), to_local(mlp_gain)
        scale_first = lax.rsqrt(
            jnp.mean(stream_in * stream_in, axis=-1, keepdims=True) + NORM_EPSILON
        )
        unit_first = stream_in * scale_first
        normed_first = (unit_first * attn_gain_l).astype(jnp.bfloat16)
        gathered_first = spread(normed_first)
        query_lin = matmul(gathered_first, query_full) + query_bias
        keyval_lin = matmul(gathered_first, head_full) + head_bias
        query = rotate(query_lin.reshape(row_count, heads_dev, HD), cosine, sine).astype(
            jnp.bfloat16
        )
        key_rows = rotate(keyval_lin[:, None, :HD], cosine, sine)[:, 0].astype(jnp.bfloat16)
        value_rows = keyval_lin[:, HD:].astype(jnp.bfloat16)
        query_b = query.reshape(half, SEG_MAX, heads_dev, HD)
        key_b, value_b = key_rows.reshape(half, SEG_MAX, HD), value_rows.reshape(half, SEG_MAX, HD)
        attn_out, log_totals = attend(query_b, key_b, value_b, allowed)
        attn_flat = attn_out.reshape(row_count, heads_dev * HD)
        middle = stream_in + collect(matmul(attn_flat, out_full_t.T))
        scale_second = lax.rsqrt(jnp.mean(middle * middle, axis=-1, keepdims=True) + NORM_EPSILON)
        unit_second = middle * scale_second
        normed_second = (unit_second * mlp_gain_l).astype(jnp.bfloat16)
        gathered_second = spread(normed_second)
        gate_lin = matmul(gathered_second, gate_full)
        up_lin = matmul(gathered_second, up_full)
        sigmoid_gate = jax.nn.sigmoid(gate_lin)
        silu_gate = gate_lin * sigmoid_gate
        hidden = (silu_gate * up_lin).astype(jnp.bfloat16)
        output = (middle + collect(matmul(hidden, down_full_t.T))).astype(jnp.bfloat16)
        cot_all = spread(cot)
        down_weight_grad = scatter_grads(cot_all.T, hidden, rows).T
        grad_hidden = matmul(cot_all, down_full_t)
        grad_gate = (
            grad_hidden * up_lin * sigmoid_gate * (1.0 + gate_lin * (1.0 - sigmoid_gate))
        ).astype(jnp.bfloat16)
        grad_up = (grad_hidden * silu_gate).astype(jnp.bfloat16)
        second_t = gathered_second.T
        gate_weight_grad = scatter_grads(second_t, grad_gate, rows)
        up_weight_grad = scatter_grads(second_t, grad_up, rows)
        grad_second = collect(matmul(grad_gate, gate_full.T) + matmul(grad_up, up_full.T))
        mlp_gain_local = jnp.sum(grad_second * unit_second, axis=0)
        weighted_second = mlp_gain_l * grad_second
        grad_middle = cot.astype(jnp.float32) + scale_second * (
            weighted_second
            - unit_second * jnp.mean(weighted_second * unit_second, axis=-1, keepdims=True)
        )
        grad_mid_all = spread(grad_middle.astype(jnp.bfloat16))
        out_weight_grad = scatter_grads(grad_mid_all.T, attn_flat, rows).T
        grad_attn = (
            matmul(grad_mid_all, out_full_t)
            .astype(jnp.bfloat16)
            .reshape(half, SEG_MAX, heads_dev, HD)
        )
        query_grad, key_grad, value_grad = attend_back(
            query_b, key_b, value_b, allowed, attn_out, log_totals, grad_attn
        )
        query_pre = rotate_back(
            query_grad.reshape(row_count, heads_dev, HD), cosine, sine
        ).reshape(row_count, heads_dev * HD)
        key_pre = rotate_back(key_grad.reshape(row_count, 1, HD), cosine, sine)[:, 0]
        share_keyval = jnp.concatenate([key_pre, value_grad.reshape(row_count, HD)], axis=1)
        query_low = query_pre.astype(jnp.bfloat16)
        share_low = share_keyval.astype(jnp.bfloat16)
        grad_first = collect(matmul(query_low, query_full.T) + matmul(share_low, head_full.T))
        both = scatter_grads(
            gathered_first.T, jnp.concatenate([query_low, share_low], axis=1), rows
        )
        query_weight_grad = both[:, :q_width]
        head_rows = both[:, q_width:]
        head_rows = head_rows + send(head_rows, "tp", core_swap)
        tp_rows = rows // n_tp
        kept = lax.dynamic_slice_in_dim(head_rows, tp_index * tp_rows, tp_rows, 0)
        gone = lax.dynamic_slice_in_dim(head_rows, (tp_index ^ 2) * tp_rows, tp_rows, 0)
        came = send(gone, "tp", chip_swap)

        def by_head(mine, theirs):
            low = jnp.where(chip == 0, mine, theirs)
            high = jnp.where(chip == 0, theirs, mine)
            return jnp.concatenate(
                [low[..., :HD], high[..., :HD], low[..., HD:], high[..., HD:]], axis=-1
            )

        keyval_weight_grad = by_head(kept, came)

        attn_gain_local = jnp.sum(grad_first * unit_first, axis=0)
        weighted_first = attn_gain_l * grad_first
        input_grad = grad_middle + scale_first * (
            weighted_first
            - unit_first * jnp.mean(weighted_first * unit_first, axis=-1, keepdims=True)
        )

        def over_fsdp(v):
            step = 1
            while step < n_fsdp:
                v = v + send(v, "fsdp", [(i, i ^ step) for i in range(n_fsdp)])
                step *= 2
            return v

        def over_tp(v):
            v = v + send(v, "tp", core_swap)
            return v + send(v, "tp", chip_swap)

        mlp_gain_grad = over_fsdp(over_tp(from_local(mlp_gain_local)))
        query_bias_local = jnp.sum(query_pre, axis=0)
        head_bias_local = jnp.sum(share_keyval, axis=0)
        biases = over_fsdp(jnp.concatenate([query_bias_local, head_bias_local]))
        query_bias_grad = biases[:q_width]
        head_bias_sum = biases[q_width:]
        head_bias_sum = head_bias_sum + send(head_bias_sum, "tp", core_swap)
        keyval_bias_grad = by_head(head_bias_sum, send(head_bias_sum, "tp", chip_swap))
        attn_gain_grad = over_fsdp(over_tp(from_local(attn_gain_local)))
        return (
            from_local(output),
            from_local(input_grad),
            attn_gain_grad,
            query_weight_grad,
            query_bias_grad,
            keyval_weight_grad,
            keyval_bias_grad,
            out_weight_grad,
            mlp_gain_grad,
            gate_weight_grad,
            up_weight_grad,
            down_weight_grad,
        )

    return local


def solution(mesh):
    in_specs = (
        P(("fsdp", "tp"), None),
        P("fsdp"),
        P(),
        P("fsdp", "tp"),
        P("tp"),
        P(("fsdp", "tp"), None),
        P(),
        P("tp", "fsdp"),
        P(),
        P("fsdp", "tp"),
        P("fsdp", "tp"),
        P("tp", "fsdp"),
        P(("fsdp", "tp"), None),
    )
    out_specs = (
        P(("fsdp", "tp"), None),
        P(("fsdp", "tp"), None),
        P(),
        P("fsdp", "tp"),
        P("tp"),
        P(("fsdp", "tp"), None),
        P(),
        P("tp", "fsdp"),
        P(),
        P("fsdp", "tp"),
        P("fsdp", "tp"),
        P("tp", "fsdp"),
    )
    local = make_local(mesh.shape["fsdp"], mesh.shape["tp"])
    return jax.shard_map(local, mesh=mesh, in_specs=in_specs, out_specs=out_specs, check_vma=False)
```
